32 devices in a mesh: gx: 4 (over z), gy: 8 (over y, x, core).
Axes of the slice: x: 2, y: 2, z: 4, core: 2. Of those that a mesh axis runs over, the one named last changes fastest.
Arguments:
- positions: float32 [3, 4, 8, 2048], P(None, 'gx', 'gy'), as said below
- velocities: float32 [3, 4, 8, 2048], P(None, 'gx', 'gy'), may hold values from -0.1 to 0.1
- bead_types: int32 [4, 8, 2048], P('gx', 'gy'), may hold values from 0 to 18, as said below
- eps_table: float32 [18, 18], replicated, may hold values from 2 to 5.6
- charges: float32 [18], replicated, may hold values from -1 to 1
- x_list: int32 [4, 8, 512], P('gx', 'gy'), may hold values from 0 to 2047, as said below
- y_list: int32 [4, 8, 512], P('gx', 'gy'), may hold values from 0 to 2047, as said below
- tiles: int32 [4, 8, 2, 112], P('gx', 'gy'), may hold values from 0 to 26, as said below
Outputs:
- new_positions: float32 [3, 4, 8, 2048], P(None, 'gx', 'gy')
- new_velocities: float32 [3, 4, 8, 2048], P(None, 'gx', 'gy')
The draws below stay inside these ranges and needn't reach their ends.
Inputs may be any that keep to these rules, and one draw needn't show every extreme that they name: `positions`: each column's slots fill a lattice of 8 x 8 x 32 sites of spacing 0.43 nm in the column's frame, one slot a site; slots 128 * c to 128 * c + 127 hold the sites of layers 2c and 2c + 1 in some order, and each bead lies within 0.03 nm of its site in every coordinate. `bead_types`: type 18 marks an empty slot; a column's empty slots are exactly its sites in layers at or above its filled height, a multiple of 2 from 2 to 32; columns (0 or 1, 0 or 1) are full. `x_list`: entry e names the slot at the site with x index e % 2, y index (e // 2) % 8 and layer e // 16. `y_list`: entry e names the slot at the site with x index e % 8, y index (e // 8) % 2 and layer e // 16. Zone clusters 0 to 24 are the own, x-import, y-import and corner clusters in the order of the zone beads; a column's real tiles come first, at most 101 of them, reached by column (0, 0), and every later slot holds the pair (25, 26).
All inputs are finite; a program needn't handle non-finite values.
Results may differ from the reference program's by a relative error of at most 0.0003.
Values sent between devices are 32-bit elements; how exact they have to be, the bound alone decides.
A program may use at most 64 MiB of HBM per device.

```python
import math
import jax
import jax.numpy as jnp
import numpy as np
from jax import lax

SIDE = 8
LAYERS = 32
NTYPES = 18
STEPS = 4
CL = 128
BEADS = 2048
STRIP = 512
NCL = 25
TILES = 112
N_GX = 4
N_GY = 8


def filled_heights(key):
    heights = 2 * jax.random.randint(jax.random.fold_in(key, 12), (N_GX, N_GY), 1, LAYERS // 2 + 1)
    full_cols = (jnp.arange(N_GX)[:, None] < 2) & (jnp.arange(N_GY)[None, :] < 2)
    return jnp.where(full_cols, LAYERS, heights).astype(jnp.int32)


def shuffle_sites(one_key):
    return jax.random.permutation(one_key, 2 * SIDE * SIDE)


def site_orders(key):
    count_all = N_GX * N_GY * (LAYERS // 2)
    keys_all = jax.random.split(jax.random.fold_in(key, 11), count_all)
    orders = jax.vmap(shuffle_sites)(keys_all)
    return orders.reshape(N_GX, N_GY, LAYERS // 2, 2 * SIDE * SIDE).astype(jnp.int32)


def slot_layers(key):
    slot_sites = jnp.argsort(site_orders(key), axis=-1)
    cluster_ids = jnp.arange(LAYERS // 2)[None, None, :, None]
    layer_ids = 2 * cluster_ids + slot_sites // (SIDE * SIDE)
    plane_ids = slot_sites % (SIDE * SIDE)
    return (layer_ids, plane_ids // SIDE, plane_ids % SIDE)


def draw_positions(key, part):
    layer_ids, y_site, x_site = slot_layers(key)
    lattice = jnp.stack([x_site, y_site, layer_ids]).astype(jnp.float32) * 0.43
    jitter_key = jax.random.fold_in(key, 13)
    jitter = jnp.clip(0.01 * jax.random.normal(jitter_key, lattice.shape, jnp.float32), -0.03, 0.03)
    return (lattice + jitter).reshape(3, N_GX, N_GY, SIDE * SIDE * LAYERS)


def draw_charges(key, part):
    sign_bits = jax.random.randint(jax.random.fold_in(key, 21), (NTYPES,), 0, 2)
    signs = 2.0 * sign_bits.astype(jnp.float32) - 1.0
    magnitude = jax.random.uniform(jax.random.fold_in(key, 22), (NTYPES,), jnp.float32, 0.5, 1.0)
    return (signs * magnitude).astype(jnp.float32)


def draw_bead_types(key, part):
    layer_ids, y_site, x_site = slot_layers(key)
    heights = filled_heights(key)
    kind_ids = jax.random.randint(jax.random.fold_in(key, 14), layer_ids.shape, 0, NTYPES)
    kind_ids = jnp.where(layer_ids < heights[:, :, None, None], kind_ids, NTYPES)
    return kind_ids.reshape(N_GX, N_GY, SIDE * SIDE * LAYERS).astype(jnp.int32)


def strip_beads(key, x_site, y_site, layer_ids):
    orders = site_orders(key)
    cluster_ids = layer_ids // 2
    site_ids = layer_ids % 2 * SIDE * SIDE + y_site * SIDE + x_site
    picked = orders[:, :, cluster_ids, site_ids]
    return (cluster_ids[None, None, :] * (2 * SIDE * SIDE) + picked).astype(jnp.int32)


def draw_x_list(key, part):
    entry = np.arange(2 * SIDE * LAYERS)
    return strip_beads(key, entry % 2, entry // 2 % SIDE, entry // (2 * SIDE))


def draw_y_list(key, part):
    entry = np.arange(2 * SIDE * LAYERS)
    return strip_beads(key, entry % SIDE, entry // SIDE % 2, entry // (2 * SIDE))


def candidate_tiles():
    spans = []
    for number in range(LAYERS // 2):
        spans.append((0, 2 * number, 2 * number + 1))
    for number in range(LAYERS // SIDE):
        spans.append((1, number * SIDE, number * SIDE + SIDE - 1))
    for number in range(LAYERS // SIDE):
        spans.append((2, number * SIDE, number * SIDE + SIDE - 1))
    corner_span = SIDE * SIDE // 2
    for number in range(LAYERS // corner_span):
        spans.append((3, number * corner_span, number * corner_span + corner_span - 1))
    listing = []
    for left_kind, right_kind in ((0, 0), (0, 1), (0, 2), (0, 3), (1, 2)):
        for left_pos, left_span in enumerate(spans):
            if left_span[0] != left_kind:
                continue
            for right_pos, right_span in enumerate(spans):
                if right_span[0] != right_kind:
                    continue
                if left_kind == right_kind and right_pos < left_pos:
                    continue
                if max(left_span[1], right_span[1]) - min(left_span[2], right_span[2]) <= 2:
                    listing.append((left_pos, right_pos, left_span[0], left_span[1], right_span[0], right_span[1]))
    return np.array(listing, dtype=np.int32)


def draw_tiles(key, part):
    listing = candidate_tiles()
    heights = filled_heights(key)
    by_zone = jnp.stack([heights, jnp.roll(heights, -1, axis=0), jnp.roll(heights, -1, axis=1), jnp.roll(jnp.roll(heights, -1, axis=0), -1, axis=1)], axis=-1)
    left_live = jnp.asarray(listing[:, 3])[None, None, :] < by_zone[:, :, listing[:, 2]]
    right_live = jnp.asarray(listing[:, 5])[None, None, :] < by_zone[:, :, listing[:, 4]]
    valid = left_live & right_live
    order_ids = jnp.argsort(jnp.where(valid, 0, 1).astype(jnp.int32), axis=-1, stable=True)
    left_ids = jnp.asarray(listing[:, 0])[order_ids]
    right_ids = jnp.asarray(listing[:, 1])[order_ids]
    counted = jnp.sum(valid.astype(jnp.int32), axis=-1, keepdims=True)
    keep_mask = jnp.arange(listing.shape[0])[None, None, :] < counted
    left_ids = jnp.where(keep_mask, left_ids, NCL)
    right_ids = jnp.where(keep_mask, right_ids, NCL + 1)
    padding = TILES - listing.shape[0]
    left_ids = jnp.concatenate([left_ids, jnp.full((N_GX, N_GY, padding), NCL, jnp.int32)], axis=-1)
    right_ids = jnp.concatenate([right_ids, jnp.full((N_GX, N_GY, padding), NCL + 1, jnp.int32)], axis=-1)
    return jnp.stack([left_ids, right_ids], axis=2).astype(jnp.int32)


def shard_levels(key, shape, cuts, least, largest):
    gain = 1.0
    for position, blocks in cuts:
        steps = jax.random.uniform(jax.random.fold_in(jax.random.fold_in(key, 6), position), (blocks,), jnp.float32, least / len(cuts), largest / len(cuts))
        gain = gain * jnp.repeat(jnp.exp(steps), shape[position] // blocks).reshape((-1,) + (1,) * (len(shape) - 1 - position))
    return gain


def noise(own_key, dims, width, limit, cuts=(), held_as=jnp.bfloat16):
    drawn = jax.random.normal(own_key, dims, jnp.float32) * width
    if len(cuts) > 0:
        drawn = shard_levels(own_key, dims, cuts, -0.22, 0.18) * drawn
    return jnp.clip(drawn, min=-limit, max=limit).astype(held_as)


def setup_inputs(seed: int = 0) -> dict:
    key_list = jax.random.split(jax.random.key(seed), 9)
    return {
        "positions": draw_positions(jax.random.fold_in(key_list[8], 71), 0),
        "velocities": noise(key_list[1], (3, N_GX, N_GY, BEADS), 0.02, 0.1, ((1, 4), (2, 8)), jnp.float32),
        "bead_types": draw_bead_types(jax.random.fold_in(key_list[8], 71), 0),
        "eps_table": jnp.clip(jnp.exp(jax.random.uniform(key_list[3], (NTYPES, NTYPES), jnp.float32, math.log(2.0), math.log(5.6))), 2.0, 5.6),
        "charges": draw_charges(jax.random.fold_in(key_list[8], 71), 0),
        "x_list": draw_x_list(jax.random.fold_in(key_list[8], 71), 0),
        "y_list": draw_y_list(jax.random.fold_in(key_list[8], 71), 0),
        "tiles": draw_tiles(jax.random.fold_in(key_list[8], 71), 0),
    }


SPACING = 0.43
CUTOFF = 1.1
SIGMA = 0.41
COULOMB = 138.935458 / 15.0
MASS = 72.0
TIME_STEP = 0.02

def pair_block(pos_a, pos_b, eps_rows, onehot_b, charge_a, charge_b, same_tile):
    width_c = pos_a.shape[2]
    offsets = []
    for component in range(3):
        offsets.append(pos_a[component][:, :, None] - pos_b[component][:, None, :])
    dist_sq = offsets[0] * offsets[0] + offsets[1] * offsets[1] + offsets[2] * offsets[2]
    diagonal = jnp.eye(width_c, dtype=jnp.float32)
    self_pair = same_tile[:, None, None] * diagonal[None]
    dist_sq = dist_sq + self_pair
    eps_pair = jnp.einsum('kni,knj->kij', eps_rows, onehot_b, precision=lax.Precision.HIGHEST)
    inv_sq = 1.0 / dist_sq
    inv_r = jnp.sqrt(inv_sq)
    sixth_pow = (SIGMA * SIGMA * inv_sq) ** 3
    lennard = 24.0 * eps_pair * (2.0 * sixth_pow * sixth_pow - sixth_pow) * inv_sq
    coulomb = COULOMB * charge_a[:, :, None] * charge_b[:, None, :] * (inv_sq * inv_r - 1.0 / CUTOFF ** 3)
    cut_ratio = dist_sq / (CUTOFF * CUTOFF)
    switch = jnp.where(cut_ratio < 1.0, (1.0 - cut_ratio) ** 2, 0.0)
    weight = (1.0 - 0.5 * same_tile)[:, None, None] * (1.0 - self_pair)
    scalar = weight * switch * (lennard + coulomb)
    on_a = jnp.stack([lax.optimization_barrier(jnp.sum(scalar * offsets[component], axis=2)) for component in range(3)])
    on_b = -jnp.stack([lax.optimization_barrier(jnp.sum(scalar * offsets[component], axis=1)) for component in range(3)])
    return (on_a, on_b)

def zone_forces(pos_zone, kind_zone, tile_pairs, eps_sym, charges):
    type_range = jnp.arange(NTYPES, dtype=jnp.int32)
    onehot = (kind_zone[:, None, :] == type_range[None, :, None]).astype(jnp.float32)
    eps_rows = jnp.einsum('nm,zmc->znc', eps_sym, onehot, precision=lax.Precision.HIGHEST)
    charge = jnp.einsum('m,zmc->zc', charges, onehot, precision=lax.Precision.HIGHEST)
    blocks = tile_pairs.reshape(2, -1, 16).transpose(1, 0, 2)

    def one_block(summed, block_pair):
        left_ids = block_pair[0]
        right_ids = block_pair[1]
        same_tile = (left_ids == right_ids).astype(jnp.float32)
        on_a, on_b = pair_block(pos_zone[:, left_ids], pos_zone[:, right_ids], eps_rows[left_ids], onehot[right_ids], charge[left_ids], charge[right_ids], same_tile)
        summed = summed.at[:, left_ids].add(on_a)
        summed = summed.at[:, right_ids].add(on_b)
        return (summed, None)
    summed, unused = lax.scan(one_block, jnp.zeros_like(pos_zone), blocks)
    return summed

def empty_clusters(cluster):
    depth = jnp.concatenate([jnp.full((cluster,), -1000.0, jnp.float32), jnp.full((cluster,), -3000.0, jnp.float32)])
    plain = jnp.zeros((2 * cluster,), jnp.float32)
    return jnp.stack([plain, plain, depth])

def scatter_one(values, index_list):
    return jnp.zeros((3, BEADS), jnp.float32).at[:, index_list].add(values)

def reference(positions, velocities, bead_types, eps_table, charges, x_list, y_list, tiles):
    coords = jnp.transpose(positions, (1, 2, 0, 3))
    speeds = jnp.transpose(velocities, (1, 2, 0, 3))
    eps_sym = 0.5 * (eps_table + eps_table.T)
    column_width = SIDE * SPACING
    shift_x = jnp.array([column_width, 0.0, 0.0], dtype=jnp.float32)[:, None]
    shift_y = jnp.array([0.0, column_width, 0.0], dtype=jnp.float32)[:, None]
    shift_both = jnp.array([column_width, column_width, 0.0], dtype=jnp.float32)[:, None]
    far_zone = jnp.broadcast_to(empty_clusters(CL), (N_GX, N_GY, 3, 2 * CL))
    far_kind = jnp.full((N_GX, N_GY, 2 * CL), NTYPES, jnp.int32)
    x_kind = jnp.take_along_axis(bead_types, x_list, axis=2)
    y_kind = jnp.take_along_axis(bead_types, y_list, axis=2)
    corner_kind = x_kind.reshape(N_GX, N_GY, LAYERS, SIDE, 2)[:, :, :, :2, :].reshape(N_GX, N_GY, 4 * LAYERS)
    zone_kind = jnp.concatenate([bead_types, jnp.roll(x_kind, -1, axis=0), jnp.roll(y_kind, -1, axis=1), jnp.roll(jnp.roll(corner_kind, -1, axis=0), -1, axis=1), far_kind], axis=2)
    devices = N_GX * N_GY
    flat_kind = zone_kind.reshape(devices, -1)
    flat_tiles = tiles.reshape(devices, 2, TILES)

    def device_forces(packed):
        zone_pos, kind_row, tile_pairs = packed
        summed = zone_forces(zone_pos.reshape(3, -1, CL), kind_row.reshape(-1, CL), tile_pairs, eps_sym, charges)
        return summed.reshape(3, -1)
    scatter_all = jax.vmap(jax.vmap(scatter_one))
    for turn_index in range(STEPS):
        x_pos = jnp.take_along_axis(coords, x_list[:, :, None, :], axis=3)
        y_pos = jnp.take_along_axis(coords, y_list[:, :, None, :], axis=3)
        corner_pos = x_pos.reshape(N_GX, N_GY, 3, LAYERS, SIDE, 2)[:, :, :, :, :2, :].reshape(N_GX, N_GY, 3, 4 * LAYERS)
        zone_x = jnp.roll(x_pos, -1, axis=0) + shift_x
        zone_y = jnp.roll(y_pos, -1, axis=1) + shift_y
        zone_c = jnp.roll(jnp.roll(corner_pos, -1, axis=0), -1, axis=1) + shift_both
        zone_pos = jnp.concatenate([coords, zone_x, zone_y, zone_c, far_zone], axis=3)
        forces = lax.map(device_forces, (zone_pos.reshape(devices, 3, -1), flat_kind, flat_tiles))
        forces = forces.reshape(N_GX, N_GY, 3, -1)
        home = forces[..., :BEADS]
        f_x = forces[..., BEADS:BEADS + STRIP]
        f_y = forces[..., BEADS + STRIP:BEADS + 2 * STRIP]
        f_c = forces[..., BEADS + 2 * STRIP:BEADS + 2 * STRIP + 4 * LAYERS]
        corner_full = jnp.zeros((N_GX, N_GY, 3, LAYERS, SIDE, 2), jnp.float32)
        corner_full = corner_full.at[:, :, :, :, :2, :].set(f_c.reshape(N_GX, N_GY, 3, LAYERS, 2, 2))
        corner_full = corner_full.reshape(N_GX, N_GY, 3, STRIP)
        back_x = jnp.roll(f_x, 1, axis=0) + jnp.roll(jnp.roll(corner_full, 1, axis=0), 1, axis=1)
        back_y = jnp.roll(f_y, 1, axis=1)
        force = home + scatter_all(back_x, x_list) + scatter_all(back_y, y_list)
        speeds = speeds + TIME_STEP / MASS * force
        coords = coords + TIME_STEP * speeds
    return (jnp.transpose(coords, (2, 0, 1, 3)), jnp.transpose(speeds, (2, 0, 1, 3)))
```

```python
import functools

import jax
import jax.numpy as jnp
from jax import lax
from jax.experimental import pallas as pl
from jax.experimental.pallas import tpu as pltpu
from jax.sharding import PartitionSpec as P

NTYPES = 18
STEPS = 4
SPACING = 0.43
CUTOFF = 1.1
SIGMA = 0.41
COULOMB = 138.935458 / 15.0
MASS = 72.0
TIME_STEP = 0.02

MESH = pl.DeviceIdType.MESH
ROWS = 16
LANES = 128
HALO = 8
NONE = 31
SIDES = [(-1, -1), (-1, 0), (-1, 1), (0, -1), (0, 1), (1, -1), (1, 0), (1, 1)]
ZONES = [(0, 0), (1, 0), (0, 1), (1, 1)]
SHIFTS = [(dx, dy) for dy in range(-2, 3) for dx in range(-2, 3)]
OFFSETS = [
    (number, dz)
    for number, (dx, dy) in enumerate(SHIFTS)
    for dz in range(-2, 3)
    if 0 < dx * dx + dy * dy + dz * dz <= 8
]


def lane_gather(values, index):
    return jnp.take_along_axis(values, index, axis=1)


def kernel(
    n_gx, n_gy, side,
    pos_ref, vel_ref, kind_ref, tile_ref, table_ref,
    out_pos_ref, out_vel_ref,
    tile_send, tile_recv, send, recv, ext, kind_ext, coef_lj, coef_q, now, speed, mix, site_ref,
    tile_sems, send_sems, recv_sems,
):
    width = side * SPACING
    my_x = lax.axis_index("gx")
    my_y = lax.axis_index("gy")

    def at(sx, sy):
        return (
            lax.rem(my_x + (sx + n_gx), n_gx),
            lax.rem(my_y + (sy + n_gy), n_gy),
        )

    barrier = pltpu.get_barrier_semaphore()
    for sx, sy in SIDES:
        pl.semaphore_signal(barrier, inc=1, device_id=at(sx, sy), device_id_type=MESH)

    lane = lax.broadcasted_iota(jnp.int32, (ROWS, LANES), 1)
    row = lax.broadcasted_iota(jnp.int32, (ROWS, LANES), 0)
    lane8 = lane[:8]
    half = lane >> 6
    y_site = (lane >> 3) & 7
    x_site = lane & 7
    low_half = lane8 < 64

    tile_send[...] = jnp.full((8, LANES), NONE - 1, jnp.int32)
    tile_send[0:2, 0 : tile_ref.shape[1]] = tile_ref[...]

    cluster = row
    sx_f = jnp.floor(pos_ref[0] * (1.0 / SPACING) + 0.5)
    sy_f = jnp.floor(pos_ref[1] * (1.0 / SPACING) + 0.5)
    sz_f = jnp.floor(pos_ref[2] * (1.0 / SPACING) + 0.5)
    site = (
        (sz_f.astype(jnp.int32) - 2 * cluster) * 64
        + sy_f.astype(jnp.int32) * 8
        + sx_f.astype(jnp.int32)
    )
    site = jnp.clip(site, 0, LANES - 1)
    site_ref[...] = site
    big_row = lax.broadcasted_iota(jnp.int32, (LANES, LANES), 0)
    row8 = row[:8]
    parts = []
    for part in range(2):
        total = jnp.zeros((8, LANES), jnp.float32)
        for sub in range(8):
            here = site[part * 8 + sub : part * 8 + sub + 1, :]
            onehot = jnp.where(big_row == here, 1.0, 0.0).astype(jnp.bfloat16)
            left = jnp.where(row8 == sub, lane8, 0).astype(jnp.float32).astype(jnp.bfloat16)
            total = total + lax.dot_general(
                left, onehot, (((1,), (1,)), ((), ())), preferred_element_type=jnp.float32
            )
        parts.append(total)
    slot = jnp.concatenate(parts, axis=0).astype(jnp.int32)

    def to_lattice(values):
        ordered = lane_gather(values, slot)
        first, second = ordered[:8], ordered[8:]
        even = jnp.where(low_half, first, pltpu.roll(second, 64, 1))
        odd = jnp.where(low_half, pltpu.roll(first, 64, 1), second)
        mix[pl.ds(0, 8, stride=2), :] = even
        mix[pl.ds(1, 8, stride=2), :] = odd
        return mix[...]

    def to_slots(values):
        mix[...] = values
        even = mix[pl.ds(0, 8, stride=2), :]
        odd = mix[pl.ds(1, 8, stride=2), :]
        first = jnp.where(low_half, even, pltpu.roll(odd, 64, 1))
        second = jnp.where(low_half, pltpu.roll(even, 64, 1), odd)
        return lane_gather(jnp.concatenate([first, second], axis=0), site_ref[...])

    for component in range(3):
        now[component] = to_lattice(pos_ref[component])
        speed[component] = to_lattice(vel_ref[component])
    kind = to_lattice(kind_ref[...].astype(jnp.float32))

    def pack_index(sx, sy):
        if sx != 0 and sy != 0:
            slot_of = lane >> 3
            inner = lane & 7
            zh, yb, xb = inner >> 2, (inner >> 1) & 1, inner & 1
        elif sx != 0:
            slot_of = lane >> 5
            inner = lane & 31
            zh, yb, xb = inner >> 4, (inner >> 1) & 7, inner & 1
        else:
            slot_of = lane >> 5
            inner = lane & 31
            zh, yb, xb = inner >> 4, (inner >> 3) & 1, inner & 7
        x_low = side - 2 if sx > 0 else 0
        y_low = side - 2 if sy > 0 else 0
        return slot_of, zh * 64 + (yb + y_low) * 8 + xb + x_low

    def unpack_index(sx, sy):
        if sx != 0 and sy != 0:
            return half * 4 + (y_site & 1) * 2 + (x_site & 1), 8
        if sx != 0:
            return half * 16 + y_site * 2 + (x_site & 1), 32
        return half * 16 + (y_site & 1) * 8 + x_site, 32

    def pack(values, sx, sy):
        slot_of, source = pack_index(sx, sy)
        packed = lane_gather(values[0], source)
        for component in range(1, len(values)):
            packed = jnp.where(slot_of == component, lane_gather(values[component], source), packed)
        return packed

    def side_copy(turn, number):
        sx, sy = SIDES[number]
        return pltpu.make_async_remote_copy(
            src_ref=send.at[turn, number],
            dst_ref=recv.at[turn, number],
            send_sem=send_sems.at[turn, number],
            recv_sem=recv_sems.at[turn, number],
            device_id=at(sx, sy),
            device_id_type=MESH,
        )

    def tile_copy(number):
        sx, sy = ZONES[number + 1]
        return pltpu.make_async_remote_copy(
            src_ref=tile_send,
            dst_ref=tile_recv.at[number],
            send_sem=tile_sems.at[0, number],
            recv_sem=tile_sems.at[1, number],
            device_id=at(sx, sy),
            device_id_type=MESH,
        )

    def image(turn, ux, uy, component):
        number = SIDES.index((-ux, -uy))
        index, stride = unpack_index(ux, uy)
        return lane_gather(recv[turn, number], index + component * stride)

    def merge_and_shift(images, dx, dy):
        merged = images[(0, 0)]
        in_x = (x_site < dx) if dx > 0 else (x_site >= side + dx)
        in_y = (y_site < dy) if dy > 0 else (y_site >= side + dy)
        ux = (dx > 0) - (dx < 0)
        uy = (dy > 0) - (dy < 0)
        if dx != 0:
            merged = jnp.where(in_x, images[(ux, 0)], merged)
        if dy != 0:
            outer = images[(0, uy)]
            if dx != 0:
                outer = jnp.where(in_x, images[(ux, uy)], outer)
            merged = jnp.where(in_y, outer, merged)
        if dx == 0 and dy == 0:
            return merged
        source = half * 64 + ((y_site + dy) & 7) * 8 + ((x_site + dx) & 7)
        return lane_gather(merged, source)

    def put_extended(ref, values):
        ref[pl.ds(HALO, ROWS), :] = values
        ref[pl.ds(0, HALO), :] = pltpu.roll(values[8:], 64, 1)
        ref[pl.ds(HALO + ROWS, HALO), :] = pltpu.roll(values[:8], 64, 1)

    def gather_images(turn, component, own):
        shift_of = (width, width, 0.0, 0.0)
        images = {(0, 0): own}
        for ux, uy in SIDES:
            got = image(turn, ux, uy, component)
            if component == 0 and ux != 0:
                got = got + ux * width
            if component == 1 and uy != 0:
                got = got + uy * width
            images[(ux, uy)] = got
        return images

    def exchange(turn, values):
        for number, (sx, sy) in enumerate(SIDES):
            send[turn, number] = pack(values, sx, sy)
        for number in range(len(SIDES)):
            side_copy(turn, number).start()

    def spread_positions(turn, own):
        for component in range(3):
            images = gather_images(turn, component, own[component])
            for number, (dx, dy) in enumerate(SHIFTS):
                put_extended(ext.at[number, component], merge_and_shift(images, dx, dy))

    pl.semaphore_wait(barrier, len(SIDES))
    own = [now[component] for component in range(3)]
    exchange(0, own + [kind])
    for number in range(3):
        tile_copy(number).start()
    for number in range(len(SIDES)):
        side_copy(0, number).wait_recv()
    for number in range(3):
        tile_copy(number).wait_recv()

    iota_small = lax.broadcasted_iota(jnp.int32, (32, LANES), 0)
    lane_small = lax.broadcasted_iota(jnp.int32, (32, LANES), 1)
    count_row = lax.broadcasted_iota(jnp.int32, (ROWS, 32), 0)
    count_lane = lax.broadcasted_iota(jnp.int32, (ROWS, 32), 1)
    nt = (((1,), (1,)), ((), ()))

    def onehot_of(condition):
        return jnp.where(condition, 1.0, 0.0).astype(jnp.bfloat16)

    tables = []
    for pair in range(2):
        table = jnp.zeros((ROWS, LANES), jnp.float32)
        for zone in (2 * pair, 2 * pair + 1):
            source = tile_send if zone == 0 else tile_recv.at[zone - 1]
            first = source[0:1, :]
            second = source[1:2, :]
            base = 32 * (zone & 1)
            small_a = onehot_of(iota_small == first)
            small_b = onehot_of(iota_small == second)
            place = big_row - base
            big_a = onehot_of((place == first) | (place == first + 64))
            big_b = onehot_of((place == second) | (place == second + 64))
            forth = lax.dot_general(small_a, big_b, nt, preferred_element_type=jnp.float32)
            back = lax.dot_general(small_b, big_a, nt, preferred_element_type=jnp.float32)
            on_diagonal = (lane_small & 63) == iota_small + base
            counts = jnp.where(on_diagonal, forth, forth + back).astype(jnp.bfloat16)
            picked = []
            for zh in range(2):
                layer = zh * ROWS + count_row
                if zone == 0:
                    which = layer >> 1
                elif zone == 1:
                    which = 16 + (layer >> 3)
                elif zone == 2:
                    which = 20 + (layer >> 3)
                else:
                    which = jnp.full_like(layer, 24)
                picked.append(
                    jnp.dot(onehot_of(count_lane == which), counts, preferred_element_type=jnp.float32)
                )
            table = table + jnp.where(half == 0, picked[0], picked[1])
        tables.append(table)

    kind_images = gather_images(0, 3, kind)
    kind_own = kind.astype(jnp.int32)
    eps_rows = [jnp.broadcast_to(table_ref[k : k + 1, :], (ROWS, LANES)) for k in range(4)]
    charge_own = lane_gather(eps_rows[3], kind_own)
    for number, (dx, dy) in enumerate(SHIFTS):
        put_extended(kind_ext.at[number], merge_and_shift(kind_images, dx, dy))

    zone_of = []
    for number, (dx, dy) in enumerate(SHIFTS):
        masks = []
        for ox, oy in ZONES:
            px, py = x_site + ox * side, y_site + oy * side
            qx, qy = px + dx, py + dy
            limit = side + 2
            inside = (px < limit) & (py < limit) & (qx >= 0) & (qx < limit) & (qy >= 0) & (qy < limit)
            in_x, in_y = qx >= side, qy >= side
            start = jnp.where(in_x, jnp.where(in_y, 24, 16), jnp.where(in_y, 20, 0))
            shift = jnp.where(in_x, jnp.where(in_y, 6, 3), jnp.where(in_y, 3, 1))
            masks.append((inside, start, shift))
        for dz in range(-2, 3):
            if (number, dz) not in OFFSETS:
                continue
            place = OFFSETS.index((number, dz))
            layer = half * ROWS + row + dz
            in_z = (layer >= 0) & (layer < 2 * ROWS)
            weight = jnp.zeros((ROWS, LANES), jnp.float32)
            for zone in range(4):
                ox, oy = ZONES[zone]
                inside, start, shift = masks[zone]
                which = jnp.where(inside & in_z, start + (layer >> shift), NONE)
                weight = weight + lane_gather(
                    tables[zone >> 1], half * 64 + 32 * (zone & 1) + which
                )
            other = kind_ext[number, pl.ds(HALO + dz, ROWS), :].astype(jnp.int32)
            pair = kind_own * (NTYPES + 1) + other
            low = pair & (LANES - 1)
            high = pair >> 7
            depth = jnp.where(
                high == 0,
                lane_gather(eps_rows[0], low),
                jnp.where(high == 1, lane_gather(eps_rows[1], low), lane_gather(eps_rows[2], low)),
            )
            coef_lj[place] = weight * depth * (24.0 * SIGMA**6)
            coef_q[place] = weight * (COULOMB * charge_own) * lane_gather(eps_rows[3], other)

    def advance(turn):
        mine = [now[component] for component in range(3)]
        spread_positions(turn, mine)
        force = [jnp.zeros((ROWS, LANES), jnp.float32) for _ in range(3)]
        for place, (number, dz) in enumerate(OFFSETS):
            apart = [mine[k] - ext[number, k, pl.ds(HALO + dz, ROWS), :] for k in range(3)]
            dist_sq = apart[0] * apart[0] + apart[1] * apart[1] + apart[2] * apart[2]
            inv_r = lax.rsqrt(dist_sq)
            inv_sq = inv_r * inv_r
            switch = jnp.maximum(1.0 - dist_sq * (1.0 / (CUTOFF * CUTOFF)), 0.0)
            inv_4 = inv_sq * inv_sq
            inv_6 = inv_4 * inv_sq
            lennard = coef_lj[place] * (inv_4 * inv_4) * (inv_6 * (2.0 * SIGMA**6) - 1.0)
            coulomb = coef_q[place] * (inv_sq * inv_r - 1.0 / CUTOFF**3)
            scalar = switch * switch * (lennard + coulomb)
            for k in range(3):
                force[k] = force[k] + scalar * apart[k]
        for k in range(3):
            new_speed = speed[k] + (TIME_STEP / MASS) * force[k]
            speed[k] = new_speed
            now[k] = mine[k] + TIME_STEP * new_speed

    def turn_body(turn, carry):
        advance(turn)
        exchange(turn + 1, [now[component] for component in range(3)])
        for number in range(len(SIDES)):
            side_copy(turn + 1, number).wait_recv()
        return carry

    lax.fori_loop(0, STEPS - 1, turn_body, 0)
    advance(STEPS - 1)
    for component in range(3):
        out_pos_ref[component] = to_slots(now[component])
        out_vel_ref[component] = to_slots(speed[component])
    for turn in range(STEPS):
        for number in range(len(SIDES)):
            side_copy(turn, number).wait_send()
    for number in range(3):
        tile_copy(number).wait_send()


def per_device(n_gx, n_gy, positions, velocities, bead_types, eps_table, charges, x_list, y_list, tiles):
    beads = positions.shape[-1]
    strip = x_list.shape[-1]
    side = 2 * beads // strip
    eps_sym = 0.5 * (eps_table + eps_table.T)
    flat = jnp.pad(eps_sym, ((0, 1), (0, 1))).reshape(-1)
    flat = jnp.pad(flat, (0, 3 * LANES - flat.shape[0])).reshape(3, LANES)
    charge_row = jnp.pad(charges, (0, LANES - charges.shape[0]))[None]
    table = jnp.concatenate([flat, charge_row, jnp.zeros((4, LANES), jnp.float32)], axis=0)
    shape = jax.ShapeDtypeStruct((3, ROWS, LANES), jnp.float32)
    vmem = pl.BlockSpec(memory_space=pltpu.VMEM)
    new_pos, new_vel = pl.pallas_call(
        functools.partial(kernel, n_gx, n_gy, side),
        out_shape=(shape, shape),
        in_specs=[vmem] * 5,
        out_specs=(vmem, vmem),
        scratch_shapes=[
            pltpu.VMEM((8, LANES), jnp.int32),
            pltpu.VMEM((3, 8, LANES), jnp.int32),
            pltpu.VMEM((STEPS, len(SIDES), ROWS, LANES), jnp.float32),
            pltpu.VMEM((STEPS, len(SIDES), ROWS, LANES), jnp.float32),
            pltpu.VMEM((len(SHIFTS), 3, ROWS + 2 * HALO, LANES), jnp.float32),
            pltpu.VMEM((len(SHIFTS), ROWS + 2 * HALO, LANES), jnp.float32),
            pltpu.VMEM((len(OFFSETS), ROWS, LANES), jnp.float32),
            pltpu.VMEM((len(OFFSETS), ROWS, LANES), jnp.float32),
            pltpu.VMEM((3, ROWS, LANES), jnp.float32),
            pltpu.VMEM((3, ROWS, LANES), jnp.float32),
            pltpu.VMEM((ROWS, LANES), jnp.float32),
            pltpu.VMEM((ROWS, LANES), jnp.int32),
            pltpu.SemaphoreType.DMA((2, 3)),
            pltpu.SemaphoreType.DMA((STEPS, len(SIDES))),
            pltpu.SemaphoreType.DMA((STEPS, len(SIDES))),
        ],
        compiler_params=pltpu.CompilerParams(collective_id=0, has_side_effects=True),
    )(
        positions.reshape(3, ROWS, LANES),
        velocities.reshape(3, ROWS, LANES),
        bead_types.reshape(ROWS, LANES),
        tiles.reshape(2, -1),
        table,
    )
    return new_pos.reshape(positions.shape), new_vel.reshape(velocities.shape)


def solution(mesh):
    return jax.shard_map(
        functools.partial(per_device, mesh.shape["gx"], mesh.shape["gy"]),
        mesh=mesh,
        in_specs=(
            P(None, "gx", "gy", None),
            P(None, "gx", "gy", None),
            P("gx", "gy", None),
            P(),
            P(),
            P("gx", "gy", None),
            P("gx", "gy", None),
            P("gx", "gy", None, None),
        ),
        out_specs=(P(None, "gx", "gy", None), P(None, "gx", "gy", None)),
        check_vma=False,
    )
```

```python
import functools

import jax
import jax.numpy as jnp
from jax import lax
from jax.experimental import pallas as pl
from jax.experimental.pallas import tpu as pltpu
from jax.sharding import PartitionSpec as P

NTYPES = 18
STEPS = 4
SPACING = 0.43
CUTOFF = 1.1
SIGMA = 0.41
COULOMB = 138.935458 / 15.0
MASS = 72.0
TIME_STEP = 0.02

MESH = pl.DeviceIdType.MESH
ROWS = 16
LANES = 128
HALO = 8
NONE = 31
SIDES = [(-1, -1), (-1, 0), (-1, 1), (0, -1), (0, 1), (1, -1), (1, 0), (1, 1)]
ZONES = [(0, 0), (1, 0), (0, 1), (1, 1)]
NEAR = [(dx, dy) for dy in range(-2, 3) for dx in range(-2, 3) if 0 < dx * dx + dy * dy <= 4]
MIDDLE = [(dx, dy) for dy in range(-2, 3) for dx in range(-2, 3) if dx * dx + dy * dy == 5]
FAR = [(dx, dy) for dy in range(-2, 3) for dx in range(-2, 3) if dx * dx + dy * dy == 8]
SHIFTS = NEAR + MIDDLE + FAR + [(0, 0)]
RUNS = [
    (0, len(NEAR), (-2, -1, 0, 1, 2), 0),
    (len(NEAR), len(MIDDLE), (-1, 0, 1), 5 * len(NEAR)),
    (len(NEAR) + len(MIDDLE), len(FAR), (0,), 5 * len(NEAR) + 3 * len(MIDDLE)),
    (len(SHIFTS) - 1, 1, (-2, -1, 1, 2), 5 * len(NEAR) + 3 * len(MIDDLE) + len(FAR)),
]
COUNT = RUNS[3][3] + 4
UNIT = SIGMA * 2.0 ** (1.0 / 6.0)
REACH = (CUTOFF / UNIT) ** 2
TAPER = (UNIT / CUTOFF) ** 4
LJ_FACTOR = 12.0 / UNIT**2 * TAPER
Q_FACTOR = COULOMB / UNIT**3 * TAPER
Q_SHIFT = (UNIT / CUTOFF) ** 3
PER_ROW = 6
STRIDE = 21
UNROLL = 2


def lane_gather(values, index):
    return jnp.take_along_axis(values, index, axis=1)


def kernel(
    n_gx, n_gy, side,
    pos_ref, vel_ref, kind_ref, tile_ref, eps_ref, charge_ref,
    out_pos_ref, out_vel_ref,
    tile_send, tile_recv, send, recv, ext, kind_ext, charge_ext, coef_lj, coef_q, now, speed, mix, site_ref, square,
    tile_sems, send_sems, recv_sems,
):
    width = side * SPACING
    my_x = lax.axis_index("gx")
    my_y = lax.axis_index("gy")

    def at(sx, sy):
        return (
            lax.rem(my_x + (sx + n_gx), n_gx),
            lax.rem(my_y + (sy + n_gy), n_gy),
        )

    barrier = pltpu.get_barrier_semaphore()
    for sx, sy in SIDES:
        pl.semaphore_signal(barrier, inc=1, device_id=at(sx, sy), device_id_type=MESH)

    lane = lax.broadcasted_iota(jnp.int32, (ROWS, LANES), 1)
    row = lax.broadcasted_iota(jnp.int32, (ROWS, LANES), 0)
    lane8 = lane[:8]
    half = lane >> 6
    y_site = (lane >> 3) & 7
    x_site = lane & 7
    low_half = lane8 < 64

    tile_send[...] = jnp.full((8, LANES), NONE - 1, jnp.int32)
    tile_send[0:2, 0 : tile_ref.shape[1]] = tile_ref[...]

    cluster = row
    sx_f = jnp.floor(pos_ref[0] * (1.0 / SPACING) + 0.5)
    sy_f = jnp.floor(pos_ref[1] * (1.0 / SPACING) + 0.5)
    sz_f = jnp.floor(pos_ref[2] * (1.0 / SPACING) + 0.5)
    site = (
        (sz_f.astype(jnp.int32) - 2 * cluster) * 64
        + sy_f.astype(jnp.int32) * 8
        + sx_f.astype(jnp.int32)
    )
    site = jnp.clip(site, 0, LANES - 1)
    site_ref[...] = site
    big_row = lax.broadcasted_iota(jnp.int32, (LANES, LANES), 0)
    row8 = row[:8]
    parts = []
    for part in range(2):
        total = jnp.zeros((8, LANES), jnp.float32)
        for sub in range(8):
            here = site[part * 8 + sub : part * 8 + sub + 1, :]
            onehot = jnp.where(big_row == here, 1.0, 0.0).astype(jnp.bfloat16)
            left = jnp.where(row8 == sub, lane8, 0).astype(jnp.float32).astype(jnp.bfloat16)
            total = total + lax.dot_general(
                left, onehot, (((1,), (1,)), ((), ())), preferred_element_type=jnp.float32
            )
        parts.append(total)
    slot = jnp.concatenate(parts, axis=0).astype(jnp.int32)

    def to_lattice(values):
        ordered = lane_gather(values, slot)
        first, second = ordered[:8], ordered[8:]
        even = jnp.where(low_half, first, pltpu.roll(second, 64, 1))
        odd = jnp.where(low_half, pltpu.roll(first, 64, 1), second)
        mix[pl.ds(0, 8, stride=2), :] = even
        mix[pl.ds(1, 8, stride=2), :] = odd
        return mix[...]

    def to_slots(values):
        mix[...] = values
        even = mix[pl.ds(0, 8, stride=2), :]
        odd = mix[pl.ds(1, 8, stride=2), :]
        first = jnp.where(low_half, even, pltpu.roll(odd, 64, 1))
        second = jnp.where(low_half, pltpu.roll(even, 64, 1), odd)
        return lane_gather(jnp.concatenate([first, second], axis=0), site_ref[...])

    for component in range(3):
        now[component] = to_lattice(pos_ref[component])
        speed[component] = to_lattice(vel_ref[component])
    kind = to_lattice(kind_ref[...].astype(jnp.float32))

    def pack_index(sx, sy):
        if sx != 0 and sy != 0:
            slot_of = lane >> 3
            inner = lane & 7
            zh, yb, xb = inner >> 2, (inner >> 1) & 1, inner & 1
        elif sx != 0:
            slot_of = lane >> 5
            inner = lane & 31
            zh, yb, xb = inner >> 4, (inner >> 1) & 7, inner & 1
        else:
            slot_of = lane >> 5
            inner = lane & 31
            zh, yb, xb = inner >> 4, (inner >> 3) & 1, inner & 7
        x_low = side - 2 if sx > 0 else 0
        y_low = side - 2 if sy > 0 else 0
        return slot_of, zh * 64 + (yb + y_low) * 8 + xb + x_low

    def unpack_index(sx, sy):
        if sx != 0 and sy != 0:
            return half * 4 + (y_site & 1) * 2 + (x_site & 1), 8
        if sx != 0:
            return half * 16 + y_site * 2 + (x_site & 1), 32
        return half * 16 + (y_site & 1) * 8 + x_site, 32

    def pack(values, sx, sy):
        slot_of, source = pack_index(sx, sy)
        packed = lane_gather(values[0], source)
        for component in range(1, len(values)):
            packed = jnp.where(slot_of == component, lane_gather(values[component], source), packed)
        return packed

    def side_copy(turn, number):
        sx, sy = SIDES[number]
        return pltpu.make_async_remote_copy(
            src_ref=send.at[turn, number],
            dst_ref=recv.at[turn, number],
            send_sem=send_sems.at[turn, number],
            recv_sem=recv_sems.at[turn, number],
            device_id=at(sx, sy),
            device_id_type=MESH,
        )

    def tile_copy(number):
        sx, sy = ZONES[number + 1]
        return pltpu.make_async_remote_copy(
            src_ref=tile_send,
            dst_ref=tile_recv.at[number],
            send_sem=tile_sems.at[0, number],
            recv_sem=tile_sems.at[1, number],
            device_id=at(sx, sy),
            device_id_type=MESH,
        )

    def image(turn, ux, uy, component):
        number = SIDES.index((-ux, -uy))
        index, stride = unpack_index(ux, uy)
        return lane_gather(recv[turn, number], index + component * stride)

    def merge_and_shift(images, dx, dy):
        merged = images[(0, 0)]
        in_x = (x_site < dx) if dx > 0 else (x_site >= side + dx)
        in_y = (y_site < dy) if dy > 0 else (y_site >= side + dy)
        ux = (dx > 0) - (dx < 0)
        uy = (dy > 0) - (dy < 0)
        if dx != 0:
            merged = jnp.where(in_x, images[(ux, 0)], merged)
        if dy != 0:
            outer = images[(0, uy)]
            if dx != 0:
                outer = jnp.where(in_x, images[(ux, uy)], outer)
            merged = jnp.where(in_y, outer, merged)
        if dx == 0 and dy == 0:
            return merged
        source = half * 64 + ((y_site + dy) & 7) * 8 + ((x_site + dx) & 7)
        return lane_gather(merged, source)

    def put_extended(ref, values):
        ref[pl.ds(HALO, ROWS), :] = values
        ref[pl.ds(0, HALO), :] = pltpu.roll(values[8:], 64, 1)
        ref[pl.ds(HALO + ROWS, HALO), :] = pltpu.roll(values[:8], 64, 1)

    def gather_images(turn, component, own):
        images = {(0, 0): own}
        for ux, uy in SIDES:
            got = image(turn, ux, uy, component)
            if component == 0 and ux != 0:
                got = got + ux * width
            if component == 1 and uy != 0:
                got = got + uy * width
            images[(ux, uy)] = got
        return images

    def exchange(turn, values):
        for number, (sx, sy) in enumerate(SIDES):
            send[turn, number] = pack(values, sx, sy)
        for number in range(len(SIDES)):
            side_copy(turn, number).start()

    def spread_positions(turn, own):
        for component in range(3):
            images = gather_images(turn, component, own[component])
            images = {key: value * (1.0 / UNIT) for key, value in images.items()}
            for number, (dx, dy) in enumerate(SHIFTS):
                put_extended(ext.at[number, component], merge_and_shift(images, dx, dy))

    square[...] = jnp.zeros((LANES, LANES), jnp.float32)
    square[0:NTYPES, 0:NTYPES] = eps_ref[...]
    padded = square[...]
    square[...] = (padded + padded.T) * (0.5 * LJ_FACTOR)
    eps_rows = []
    for k in range(NTYPES // PER_ROW):
        flat = square[PER_ROW * k : PER_ROW * k + 1, :]
        for m in range(1, PER_ROW):
            flat = flat + pltpu.roll(square[PER_ROW * k + m : PER_ROW * k + m + 1, :], STRIDE * m, 1)
        eps_rows.append(jnp.broadcast_to(flat, (ROWS, LANES)))
    mix[0:1, :] = jnp.zeros((1, LANES), jnp.float32)
    mix[0:1, 0:NTYPES] = charge_ref[...]
    charge_row = jnp.broadcast_to(mix[0:1, :], (ROWS, LANES))

    pl.semaphore_wait(barrier, len(SIDES))
    own = [now[component] for component in range(3)]
    exchange(0, own + [kind])
    for number in range(3):
        tile_copy(number).start()
    for number in range(len(SIDES)):
        side_copy(0, number).wait_recv()
    for number in range(3):
        tile_copy(number).wait_recv()

    iota_small = lax.broadcasted_iota(jnp.int32, (32, LANES), 0)
    lane_small = lax.broadcasted_iota(jnp.int32, (32, LANES), 1)
    count_row = lax.broadcasted_iota(jnp.int32, (ROWS, 32), 0)
    count_lane = lax.broadcasted_iota(jnp.int32, (ROWS, 32), 1)
    nt = (((1,), (1,)), ((), ()))

    def onehot_of(condition):
        return jnp.where(condition, 1.0, 0.0).astype(jnp.bfloat16)

    tables = []
    for pair in range(2):
        table = jnp.zeros((ROWS, LANES), jnp.float32)
        for zone in (2 * pair, 2 * pair + 1):
            source = tile_send if zone == 0 else tile_recv.at[zone - 1]
            first = source[0:1, :]
            second = source[1:2, :]
            base = 32 * (zone & 1)
            small_a = onehot_of(iota_small == first)
            small_b = onehot_of(iota_small == second)
            place = big_row - base
            big_a = onehot_of((place == first) | (place == first + 64))
            big_b = onehot_of((place == second) | (place == second + 64))
            forth = lax.dot_general(small_a, big_b, nt, preferred_element_type=jnp.float32)
            back = lax.dot_general(small_b, big_a, nt, preferred_element_type=jnp.float32)
            on_diagonal = (lane_small & 63) == iota_small + base
            counts = jnp.where(on_diagonal, forth, forth + back).astype(jnp.bfloat16)
            picked = []
            for zh in range(2):
                layer = zh * ROWS + count_row
                if zone == 0:
                    which = layer >> 1
                elif zone == 1:
                    which = 16 + (layer >> 3)
                elif zone == 2:
                    which = 20 + (layer >> 3)
                else:
                    which = jnp.full_like(layer, 24)
                picked.append(
                    jnp.dot(onehot_of(count_lane == which), counts, preferred_element_type=jnp.float32)
                )
            table = table + jnp.where(half == 0, picked[0], picked[1])
        tables.append(table)

    cat_x, cat_y = (lane >> 2) & 3, lane & 3
    weight_of = {}
    for dz in range(-2, 3):
        layer = half * ROWS + row + dz
        in_z = (layer >= 0) & (layer < 2 * ROWS)
        total = jnp.zeros((ROWS, LANES), jnp.float32)
        for zone, (ox, oy) in enumerate(ZONES):
            on_x = (cat_x >= 2) if ox else (cat_x <= 2)
            on_y = (cat_y >= 2) if oy else (cat_y <= 2)
            in_x = cat_x == (2 if ox else 1)
            in_y = cat_y == (2 if oy else 1)
            start = jnp.where(in_x, jnp.where(in_y, 24, 16), jnp.where(in_y, 20, 0))
            shift = jnp.where(in_x, jnp.where(in_y, 6, 3), jnp.where(in_y, 3, 1))
            which = jnp.where(on_x & on_y & in_z, start + (layer >> shift), NONE)
            total = total + lane_gather(tables[zone >> 1], half * 64 + 32 * (zone & 1) + which)
        weight_of[dz] = total

    def category(site, step):
        other = site + step
        return jnp.where(
            other >= side, 1, jnp.where(other < 0, 3, jnp.where((site < 2) & (other < 2), 2, 0))
        )

    kind_images = gather_images(0, 3, kind)
    kind_images = {key: value.astype(jnp.int32) for key, value in kind_images.items()}
    charge_images = {key: lane_gather(charge_row, value) for key, value in kind_images.items()}
    kind_own = kind_images[(0, 0)]
    kind_row = sum((kind_own >= PER_ROW * k).astype(jnp.int32) for k in range(1, 4))
    kind_base = (kind_own - PER_ROW * kind_row) * STRIDE
    in_row = [kind_row == k for k in range(3)]
    for number, (dx, dy) in enumerate(SHIFTS):
        put_extended(kind_ext.at[number], merge_and_shift(kind_images, dx, dy))
        put_extended(charge_ext.at[number], merge_and_shift(charge_images, dx, dy))
    charge_own = charge_images[(0, 0)] * Q_FACTOR
    for first, length, depths, base in RUNS:
        for sub in range(length):
            number = first + sub
            dx, dy = SHIFTS[number]
            chosen = half * 64 + category(x_site, dx) * 4 + category(y_site, dy)
            for turn, dz in enumerate(depths):
                place = base + sub * len(depths) + turn
                weight = lane_gather(weight_of[dz], chosen)
                rows = pl.ds(HALO + dz, ROWS)
                low = kind_base + kind_ext[number, rows, :]
                depth = jnp.where(in_row[2], lane_gather(eps_rows[2], low), 0.0)
                depth = jnp.where(in_row[1], lane_gather(eps_rows[1], low), depth)
                depth = jnp.where(in_row[0], lane_gather(eps_rows[0], low), depth)
                coef_lj[place] = weight * depth
                coef_q[place] = weight * (charge_own * charge_ext[number, rows, :])

    def add_pair(scaled, force, place, number, dz):
        apart = [scaled[k] - ext[number, k, pl.ds(HALO + dz, ROWS), :] for k in range(3)]
        dist_sq = apart[0] * apart[0] + apart[1] * apart[1] + apart[2] * apart[2]
        inv_r = lax.rsqrt(dist_sq)
        inv_sq = inv_r * inv_r
        taper = jnp.maximum(REACH - dist_sq, 0.0)
        inv_4 = inv_sq * inv_sq
        inv_6 = inv_4 * inv_sq
        lennard = coef_lj[place] * (inv_4 * inv_4) * (inv_6 - 1.0)
        coulomb = coef_q[place] * (inv_sq * inv_r - Q_SHIFT)
        scalar = taper * taper * (lennard + coulomb)
        return [force[k] + scalar * apart[k] for k in range(3)]

    def advance(turn):
        mine = [now[component] for component in range(3)]
        spread_positions(turn, mine)
        scaled = [mine[k] * (1.0 / UNIT) for k in range(3)]
        force = [jnp.zeros((ROWS, LANES), jnp.float32) for _ in range(3)]
        for first, length, depths, base in RUNS:
            def run(sub, held):
                held = list(held)
                for which, dz in enumerate(depths):
                    held = add_pair(scaled, held, base + sub * len(depths) + which, first + sub, dz)
                return tuple(held)
            if length * len(depths) > 4:
                force = list(lax.fori_loop(0, length, run, tuple(force), unroll=UNROLL))
            else:
                for sub in range(length):
                    force = list(run(sub, force))
        for k in range(3):
            new_speed = speed[k] + (TIME_STEP / MASS * UNIT) * force[k]
            speed[k] = new_speed
            now[k] = mine[k] + TIME_STEP * new_speed

    def turn_body(turn, carry):
        advance(turn)
        exchange(turn + 1, [now[component] for component in range(3)])
        for number in range(len(SIDES)):
            side_copy(turn + 1, number).wait_recv()
        return carry

    lax.fori_loop(0, STEPS - 1, turn_body, 0)
    advance(STEPS - 1)
    for component in range(3):
        out_pos_ref[component] = to_slots(now[component])
        out_vel_ref[component] = to_slots(speed[component])
    for turn in range(STEPS):
        for number in range(len(SIDES)):
            side_copy(turn, number).wait_send()
    for number in range(3):
        tile_copy(number).wait_send()


def per_device(n_gx, n_gy, positions, velocities, bead_types, eps_table, charges, x_list, y_list, tiles):
    beads = positions.shape[-1]
    strip = x_list.shape[-1]
    side = 2 * beads // strip
    shape = jax.ShapeDtypeStruct((3, ROWS, LANES), jnp.float32)
    vmem = pl.BlockSpec(memory_space=pltpu.VMEM)
    new_pos, new_vel = pl.pallas_call(
        functools.partial(kernel, n_gx, n_gy, side),
        out_shape=(shape, shape),
        in_specs=[vmem] * 6,
        out_specs=(vmem, vmem),
        scratch_shapes=[
            pltpu.VMEM((8, LANES), jnp.int32),
            pltpu.VMEM((3, 8, LANES), jnp.int32),
            pltpu.VMEM((STEPS, len(SIDES), ROWS, LANES), jnp.float32),
            pltpu.VMEM((STEPS, len(SIDES), ROWS, LANES), jnp.float32),
            pltpu.VMEM((len(SHIFTS), 3, ROWS + 2 * HALO, LANES), jnp.float32),
            pltpu.VMEM((len(SHIFTS), ROWS + 2 * HALO, LANES), jnp.int32),
            pltpu.VMEM((len(SHIFTS), ROWS + 2 * HALO, LANES), jnp.float32),
            pltpu.VMEM((COUNT, ROWS, LANES), jnp.float32),
            pltpu.VMEM((COUNT, ROWS, LANES), jnp.float32),
            pltpu.VMEM((3, ROWS, LANES), jnp.float32),
            pltpu.VMEM((3, ROWS, LANES), jnp.float32),
            pltpu.VMEM((ROWS, LANES), jnp.float32),
            pltpu.VMEM((ROWS, LANES), jnp.int32),
            pltpu.VMEM((LANES, LANES), jnp.float32),
            pltpu.SemaphoreType.DMA((2, 3)),
            pltpu.SemaphoreType.DMA((STEPS, len(SIDES))),
            pltpu.SemaphoreType.DMA((STEPS, len(SIDES))),
        ],
        compiler_params=pltpu.CompilerParams(collective_id=0, has_side_effects=True),
    )(
        positions.reshape(3, ROWS, LANES),
        velocities.reshape(3, ROWS, LANES),
        bead_types.reshape(ROWS, LANES),
        tiles.reshape(2, -1),
        eps_table,
        charges[None],
    )
    return new_pos.reshape(positions.shape), new_vel.reshape(velocities.shape)


def solution(mesh):
    return jax.shard_map(
        functools.partial(per_device, mesh.shape["gx"], mesh.shape["gy"]),
        mesh=mesh,
        in_specs=(
            P(None, "gx", "gy", None),
            P(None, "gx", "gy", None),
            P("gx", "gy", None),
            P(),
            P(),
            P("gx", "gy", None),
            P("gx", "gy", None),
            P("gx", "gy", None, None),
        ),
        out_specs=(P(None, "gx", "gy", None), P(None, "gx", "gy", None)),
        check_vma=False,
    )
```

```python
import functools

import jax
import jax.numpy as jnp
from jax import lax
from jax.experimental import pallas as pl
from jax.experimental.pallas import tpu as pltpu
from jax.sharding import PartitionSpec as P

NTYPES = 18
STEPS = 4
SPACING = 0.43
CUTOFF = 1.1
SIGMA = 0.41
COULOMB = 138.935458 / 15.0
MASS = 72.0
TIME_STEP = 0.02

MESH = pl.DeviceIdType.MESH
ROWS = 16
LANES = 128
HALO = 8
NONE = 31
SIDES = [(-1, -1), (-1, 0), (-1, 1), (0, -1), (0, 1), (1, -1), (1, 0), (1, 1)]
ZONES = [(0, 0), (1, 0), (0, 1), (1, 1)]
NEAR = [(dx, dy) for dy in range(-2, 3) for dx in range(-2, 3) if 0 < dx * dx + dy * dy <= 4]
MIDDLE = [(dx, dy) for dy in range(-2, 3) for dx in range(-2, 3) if dx * dx + dy * dy == 5]
FAR = [(dx, dy) for dy in range(-2, 3) for dx in range(-2, 3) if dx * dx + dy * dy == 8]
SHIFTS = NEAR + MIDDLE + FAR + [(0, 0)]
RUNS = [
    (0, len(NEAR), (-2, -1, 0, 1, 2), 0),
    (len(NEAR), len(MIDDLE), (-1, 0, 1), 5 * len(NEAR)),
    (len(NEAR) + len(MIDDLE), len(FAR), (0,), 5 * len(NEAR) + 3 * len(MIDDLE)),
    (len(SHIFTS) - 1, 1, (-2, -1, 1, 2), 5 * len(NEAR) + 3 * len(MIDDLE) + len(FAR)),
]
COUNT = RUNS[3][3] + 4
UNIT = SIGMA * 2.0 ** (1.0 / 6.0)
REACH = (CUTOFF / UNIT) ** 2
TAPER = (UNIT / CUTOFF) ** 4
LJ_FACTOR = 12.0 / UNIT**2 * TAPER
Q_FACTOR = COULOMB / UNIT**3 * TAPER
Q_SHIFT = (UNIT / CUTOFF) ** 3
PER_ROW = 6
STRIDE = 21
AHEAD = 3


def lane_gather(values, index):
    return jnp.take_along_axis(values, index, axis=1)


def kernel(
    n_gx, n_gy, side,
    pos_ref, vel_ref, kind_ref, tile_ref, eps_ref, charge_ref,
    out_pos_ref, out_vel_ref,
    tile_send, tile_recv, send, recv, ext, kind_ext, charge_ext, coef_lj, coef_q, now, speed, mix, site_ref, square,
    tile_sems, send_sems, recv_sems,
):
    width = side * SPACING
    my_x = lax.axis_index("gx")
    my_y = lax.axis_index("gy")

    def at(sx, sy):
        return (
            lax.rem(my_x + (sx + n_gx), n_gx),
            lax.rem(my_y + (sy + n_gy), n_gy),
        )

    barrier = pltpu.get_barrier_semaphore()
    for sx, sy in SIDES:
        pl.semaphore_signal(barrier, inc=1, device_id=at(sx, sy), device_id_type=MESH)

    lane = lax.broadcasted_iota(jnp.int32, (ROWS, LANES), 1)
    row = lax.broadcasted_iota(jnp.int32, (ROWS, LANES), 0)
    lane8 = lane[:8]
    half = lane >> 6
    y_site = (lane >> 3) & 7
    x_site = lane & 7
    low_half = lane8 < 64

    tile_send[...] = jnp.full((8, LANES), NONE - 1, jnp.int32)
    tile_send[0:2, 0 : tile_ref.shape[1]] = tile_ref[...]

    cluster = row
    sx_f = jnp.floor(pos_ref[0] * (1.0 / SPACING) + 0.5)
    sy_f = jnp.floor(pos_ref[1] * (1.0 / SPACING) + 0.5)
    sz_f = jnp.floor(pos_ref[2] * (1.0 / SPACING) + 0.5)
    site = (
        (sz_f.astype(jnp.int32) - 2 * cluster) * 64
        + sy_f.astype(jnp.int32) * 8
        + sx_f.astype(jnp.int32)
    )
    site = jnp.clip(site, 0, LANES - 1)
    site_ref[...] = site
    big_row = lax.broadcasted_iota(jnp.int32, (LANES, LANES), 0)
    row8 = row[:8]
    parts = []
    for part in range(2):
        total = jnp.zeros((8, LANES), jnp.float32)
        for sub in range(8):
            here = site[part * 8 + sub : part * 8 + sub + 1, :]
            onehot = jnp.where(big_row == here, 1.0, 0.0).astype(jnp.bfloat16)
            left = jnp.where(row8 == sub, lane8, 0).astype(jnp.float32).astype(jnp.bfloat16)
            total = total + lax.dot_general(
                left, onehot, (((1,), (1,)), ((), ())), preferred_element_type=jnp.float32
            )
        parts.append(total)
    slot = jnp.concatenate(parts, axis=0).astype(jnp.int32)

    def to_lattice(values):
        ordered = lane_gather(values, slot)
        first, second = ordered[:8], ordered[8:]
        even = jnp.where(low_half, first, pltpu.roll(second, 64, 1))
        odd = jnp.where(low_half, pltpu.roll(first, 64, 1), second)
        mix[pl.ds(0, 8, stride=2), :] = even
        mix[pl.ds(1, 8, stride=2), :] = odd
        return mix[...]

    def to_slots(values):
        mix[...] = values
        even = mix[pl.ds(0, 8, stride=2), :]
        odd = mix[pl.ds(1, 8, stride=2), :]
        first = jnp.where(low_half, even, pltpu.roll(odd, 64, 1))
        second = jnp.where(low_half, pltpu.roll(even, 64, 1), odd)
        return lane_gather(jnp.concatenate([first, second], axis=0), site_ref[...])

    for component in range(3):
        now[component] = to_lattice(pos_ref[component])
        speed[component] = to_lattice(vel_ref[component])
    kind = to_lattice(kind_ref[...].astype(jnp.float32))

    def pack_index(sx, sy):
        if sx != 0 and sy != 0:
            slot_of = lane >> 3
            inner = lane & 7
            zh, yb, xb = inner >> 2, (inner >> 1) & 1, inner & 1
        elif sx != 0:
            slot_of = lane >> 5
            inner = lane & 31
            zh, yb, xb = inner >> 4, (inner >> 1) & 7, inner & 1
        else:
            slot_of = lane >> 5
            inner = lane & 31
            zh, yb, xb = inner >> 4, (inner >> 3) & 1, inner & 7
        x_low = side - 2 if sx > 0 else 0
        y_low = side - 2 if sy > 0 else 0
        return slot_of, zh * 64 + (yb + y_low) * 8 + xb + x_low

    def unpack_index(sx, sy):
        if sx != 0 and sy != 0:
            return half * 4 + (y_site & 1) * 2 + (x_site & 1), 8
        if sx != 0:
            return half * 16 + y_site * 2 + (x_site & 1), 32
        return half * 16 + (y_site & 1) * 8 + x_site, 32

    def pack(values, sx, sy):
        slot_of, source = pack_index(sx, sy)
        packed = lane_gather(values[0], source)
        for component in range(1, len(values)):
            packed = jnp.where(slot_of == component, lane_gather(values[component], source), packed)
        return packed

    def side_copy(turn, number):
        sx, sy = SIDES[number]
        return pltpu.make_async_remote_copy(
            src_ref=send.at[turn, number],
            dst_ref=recv.at[turn, number],
            send_sem=send_sems.at[turn, number],
            recv_sem=recv_sems.at[turn, number],
            device_id=at(sx, sy),
            device_id_type=MESH,
        )

    def tile_copy(number):
        sx, sy = ZONES[number + 1]
        return pltpu.make_async_remote_copy(
            src_ref=tile_send,
            dst_ref=tile_recv.at[number],
            send_sem=tile_sems.at[0, number],
            recv_sem=tile_sems.at[1, number],
            device_id=at(sx, sy),
            device_id_type=MESH,
        )

    def image(turn, ux, uy, component):
        number = SIDES.index((-ux, -uy))
        index, stride = unpack_index(ux, uy)
        return lane_gather(recv[turn, number], index + component * stride)

    def merge_and_shift(images, dx, dy):
        merged = images[(0, 0)]
        in_x = (x_site < dx) if dx > 0 else (x_site >= side + dx)
        in_y = (y_site < dy) if dy > 0 else (y_site >= side + dy)
        ux = (dx > 0) - (dx < 0)
        uy = (dy > 0) - (dy < 0)
        if dx != 0:
            merged = jnp.where(in_x, images[(ux, 0)], merged)
        if dy != 0:
            outer = images[(0, uy)]
            if dx != 0:
                outer = jnp.where(in_x, images[(ux, uy)], outer)
            merged = jnp.where(in_y, outer, merged)
        if dx == 0 and dy == 0:
            return merged
        source = half * 64 + ((y_site + dy) & 7) * 8 + ((x_site + dx) & 7)
        return lane_gather(merged, source)

    def put_extended(ref, values):
        ref[pl.ds(HALO, ROWS), :] = values
        turned = pltpu.roll(jnp.where(row8 < 4, values[:8], values[8:]), 64, 1)
        ref[pl.ds(0, HALO), :] = turned
        ref[pl.ds(HALO + ROWS, HALO), :] = turned

    def gather_images(turn, component, own):
        images = {(0, 0): own}
        for ux, uy in SIDES:
            got = image(turn, ux, uy, component)
            if component == 0 and ux != 0:
                got = got + ux * width
            if component == 1 and uy != 0:
                got = got + uy * width
            images[(ux, uy)] = got
        return images

    def exchange(turn, values):
        for number, (sx, sy) in enumerate(SIDES):
            send[turn, number] = pack(values, sx, sy)
        for number in range(len(SIDES)):
            side_copy(turn, number).start()

    def spread_position(images, number):
        dx, dy = SHIFTS[number]
        for component in range(3):
            put_extended(ext.at[number, component], merge_and_shift(images[component], dx, dy))

    square[...] = jnp.zeros((LANES, LANES), jnp.float32)
    square[0:NTYPES, 0:NTYPES] = eps_ref[...]
    padded = square[...]
    square[...] = (padded + padded.T) * (0.5 * LJ_FACTOR)
    eps_rows = []
    for k in range(NTYPES // PER_ROW):
        flat = square[PER_ROW * k : PER_ROW * k + 1, :]
        for m in range(1, PER_ROW):
            flat = flat + pltpu.roll(square[PER_ROW * k + m : PER_ROW * k + m + 1, :], STRIDE * m, 1)
        eps_rows.append(jnp.broadcast_to(flat, (ROWS, LANES)))
    mix[0:1, :] = jnp.zeros((1, LANES), jnp.float32)
    mix[0:1, 0:NTYPES] = charge_ref[...]
    charge_row = jnp.broadcast_to(mix[0:1, :], (ROWS, LANES))

    pl.semaphore_wait(barrier, len(SIDES))
    own = [now[component] for component in range(3)]
    exchange(0, own + [kind])
    for number in range(3):
        tile_copy(number).start()
    for number in range(len(SIDES)):
        side_copy(0, number).wait_recv()
    for number in range(3):
        tile_copy(number).wait_recv()

    iota_small = lax.broadcasted_iota(jnp.int32, (32, LANES), 0)
    lane_small = lax.broadcasted_iota(jnp.int32, (32, LANES), 1)
    count_row = lax.broadcasted_iota(jnp.int32, (ROWS, 32), 0)
    count_lane = lax.broadcasted_iota(jnp.int32, (ROWS, 32), 1)
    nt = (((1,), (1,)), ((), ()))

    def onehot_of(condition):
        return jnp.where(condition, 1.0, 0.0).astype(jnp.bfloat16)

    tables = []
    for pair in range(2):
        table = jnp.zeros((ROWS, LANES), jnp.float32)
        for zone in (2 * pair, 2 * pair + 1):
            source = tile_send if zone == 0 else tile_recv.at[zone - 1]
            first = source[0:1, :]
            second = source[1:2, :]
            base = 32 * (zone & 1)
            small_a = onehot_of(iota_small == first)
            small_b = onehot_of(iota_small == second)
            place = big_row - base
            big_a = onehot_of((place == first) | (place == first + 64))
            big_b = onehot_of((place == second) | (place == second + 64))
            forth = lax.dot_general(small_a, big_b, nt, preferred_element_type=jnp.float32)
            back = lax.dot_general(small_b, big_a, nt, preferred_element_type=jnp.float32)
            on_diagonal = (lane_small & 63) == iota_small + base
            counts = jnp.where(on_diagonal, forth, forth + back).astype(jnp.bfloat16)
            picked = []
            for zh in range(2):
                layer = zh * ROWS + count_row
                if zone == 0:
                    which = layer >> 1
                elif zone == 1:
                    which = 16 + (layer >> 3)
                elif zone == 2:
                    which = 20 + (layer >> 3)
                else:
                    which = jnp.full_like(layer, 24)
                picked.append(
                    jnp.dot(onehot_of(count_lane == which), counts, preferred_element_type=jnp.float32)
                )
            table = table + jnp.where(half == 0, picked[0], picked[1])
        tables.append(table)

    cat_x, cat_y = (lane >> 2) & 3, lane & 3
    weight_of = {}
    for dz in range(-2, 3):
        layer = half * ROWS + row + dz
        in_z = (layer >= 0) & (layer < 2 * ROWS)
        total = jnp.zeros((ROWS, LANES), jnp.float32)
        for zone, (ox, oy) in enumerate(ZONES):
            on_x = (cat_x >= 2) if ox else (cat_x <= 2)
            on_y = (cat_y >= 2) if oy else (cat_y <= 2)
            in_x = cat_x == (2 if ox else 1)
            in_y = cat_y == (2 if oy else 1)
            start = jnp.where(in_x, jnp.where(in_y, 24, 16), jnp.where(in_y, 20, 0))
            shift = jnp.where(in_x, jnp.where(in_y, 6, 3), jnp.where(in_y, 3, 1))
            which = jnp.where(on_x & on_y & in_z, start + (layer >> shift), NONE)
            total = total + lane_gather(tables[zone >> 1], half * 64 + 32 * (zone & 1) + which)
        weight_of[dz] = total

    def category(site, step):
        other = site + step
        return jnp.where(
            other >= side, 1, jnp.where(other < 0, 3, jnp.where((site < 2) & (other < 2), 2, 0))
        )

    kind_images = gather_images(0, 3, kind)
    kind_images = {key: value.astype(jnp.int32) for key, value in kind_images.items()}
    charge_images = {key: lane_gather(charge_row, value) for key, value in kind_images.items()}
    kind_own = kind_images[(0, 0)]
    kind_row = sum((kind_own >= PER_ROW * k).astype(jnp.int32) for k in range(1, 4))
    kind_base = (kind_own - PER_ROW * kind_row) * STRIDE
    in_row = [kind_row == k for k in range(3)]
    def spread_kind(number):
        dx, dy = SHIFTS[number]
        put_extended(kind_ext.at[number], merge_and_shift(kind_images, dx, dy))
        put_extended(charge_ext.at[number], merge_and_shift(charge_images, dx, dy))

    for number in range(AHEAD):
        spread_kind(number)
    charge_own = charge_images[(0, 0)] * Q_FACTOR
    for first, length, depths, base in RUNS:
        for sub in range(length):
            number = first + sub
            if number + AHEAD < len(SHIFTS):
                spread_kind(number + AHEAD)
            dx, dy = SHIFTS[number]
            chosen = half * 64 + category(x_site, dx) * 4 + category(y_site, dy)
            for turn, dz in enumerate(depths):
                place = base + sub * len(depths) + turn
                weight = lane_gather(weight_of[dz], chosen)
                rows = pl.ds(HALO + dz, ROWS)
                low = kind_base + kind_ext[number, rows, :]
                depth = jnp.where(in_row[2], lane_gather(eps_rows[2], low), 0.0)
                depth = jnp.where(in_row[1], lane_gather(eps_rows[1], low), depth)
                depth = jnp.where(in_row[0], lane_gather(eps_rows[0], low), depth)
                coef_lj[place] = weight * depth
                coef_q[place] = weight * (charge_own * charge_ext[number, rows, :])

    def add_pair(scaled, force, place, number, dz):
        apart = [scaled[k] - ext[number, k, pl.ds(HALO + dz, ROWS), :] for k in range(3)]
        dist_sq = apart[0] * apart[0] + apart[1] * apart[1] + apart[2] * apart[2]
        inv_r = lax.rsqrt(dist_sq)
        inv_sq = inv_r * inv_r
        taper = jnp.maximum(REACH - dist_sq, 0.0)
        inv_4 = inv_sq * inv_sq
        inv_6 = inv_4 * inv_sq
        lennard = coef_lj[place] * (inv_4 * inv_4) * (inv_6 - 1.0)
        coulomb = coef_q[place] * (inv_sq * inv_r - Q_SHIFT)
        scalar = taper * taper * (lennard + coulomb)
        return [force[k] + scalar * apart[k] for k in range(3)]

    def advance(turn):
        mine = [now[component] for component in range(3)]
        images = []
        for component in range(3):
            found = gather_images(turn, component, mine[component])
            images.append({key: value * (1.0 / UNIT) for key, value in found.items()})
        scaled = [images[k][(0, 0)] for k in range(3)]
        force = [jnp.zeros((ROWS, LANES), jnp.float32) for _ in range(3)]
        for number in range(AHEAD):
            spread_position(images, number)
        for first, length, depths, base in RUNS:
            for sub in range(length):
                number = first + sub
                if number + AHEAD < len(SHIFTS):
                    spread_position(images, number + AHEAD)
                for which, dz in enumerate(depths):
                    force = add_pair(scaled, force, base + sub * len(depths) + which, number, dz)
        for k in range(3):
            new_speed = speed[k] + (TIME_STEP / MASS * UNIT) * force[k]
            speed[k] = new_speed
            now[k] = mine[k] + TIME_STEP * new_speed

    def turn_body(turn, carry):
        advance(turn)
        exchange(turn + 1, [now[component] for component in range(3)])
        for number in range(len(SIDES)):
            side_copy(turn + 1, number).wait_recv()
        return carry

    lax.fori_loop(0, STEPS - 1, turn_body, 0)
    advance(STEPS - 1)
    for component in range(3):
        out_pos_ref[component] = to_slots(now[component])
        out_vel_ref[component] = to_slots(speed[component])
    for turn in range(STEPS):
        for number in range(len(SIDES)):
            side_copy(turn, number).wait_send()
    for number in range(3):
        tile_copy(number).wait_send()


def per_device(n_gx, n_gy, positions, velocities, bead_types, eps_table, charges, x_list, y_list, tiles):
    beads = positions.shape[-1]
    strip = x_list.shape[-1]
    side = 2 * beads // strip
    shape = jax.ShapeDtypeStruct((3, ROWS, LANES), jnp.float32)
    vmem = pl.BlockSpec(memory_space=pltpu.VMEM)
    new_pos, new_vel = pl.pallas_call(
        functools.partial(kernel, n_gx, n_gy, side),
        out_shape=(shape, shape),
        in_specs=[vmem] * 6,
        out_specs=(vmem, vmem),
        scratch_shapes=[
            pltpu.VMEM((8, LANES), jnp.int32),
            pltpu.VMEM((3, 8, LANES), jnp.int32),
            pltpu.VMEM((STEPS, len(SIDES), ROWS, LANES), jnp.float32),
            pltpu.VMEM((STEPS, len(SIDES), ROWS, LANES), jnp.float32),
            pltpu.VMEM((len(SHIFTS), 3, ROWS + 2 * HALO, LANES), jnp.float32),
            pltpu.VMEM((len(SHIFTS), ROWS + 2 * HALO, LANES), jnp.int32),
            pltpu.VMEM((len(SHIFTS), ROWS + 2 * HALO, LANES), jnp.float32),
            pltpu.VMEM((COUNT, ROWS, LANES), jnp.float32),
            pltpu.VMEM((COUNT, ROWS, LANES), jnp.float32),
            pltpu.VMEM((3, ROWS, LANES), jnp.float32),
            pltpu.VMEM((3, ROWS, LANES), jnp.float32),
            pltpu.VMEM((ROWS, LANES), jnp.float32),
            pltpu.VMEM((ROWS, LANES), jnp.int32),
            pltpu.VMEM((LANES, LANES), jnp.float32),
            pltpu.SemaphoreType.DMA((2, 3)),
            pltpu.SemaphoreType.DMA((STEPS, len(SIDES))),
            pltpu.SemaphoreType.DMA((STEPS, len(SIDES))),
        ],
        compiler_params=pltpu.CompilerParams(collective_id=0, has_side_effects=True),
    )(
        positions.reshape(3, ROWS, LANES),
        velocities.reshape(3, ROWS, LANES),
        bead_types.reshape(ROWS, LANES),
        tiles.reshape(2, -1),
        eps_table,
        charges[None],
    )
    return new_pos.reshape(positions.shape), new_vel.reshape(velocities.shape)


def solution(mesh):
    return jax.shard_map(
        functools.partial(per_device, mesh.shape["gx"], mesh.shape["gy"]),
        mesh=mesh,
        in_specs=(
            P(None, "gx", "gy", None),
            P(None, "gx", "gy", None),
            P("gx", "gy", None),
            P(),
            P(),
            P("gx", "gy", None),
            P("gx", "gy", None),
            P("gx", "gy", None, None),
        ),
        out_specs=(P(None, "gx", "gy", None), P(None, "gx", "gy", None)),
        check_vma=False,
    )
```

```python
import functools

import jax
import jax.numpy as jnp
from jax import lax
from jax.experimental import pallas as pl
from jax.experimental.pallas import tpu as pltpu
from jax.sharding import PartitionSpec as P

NTYPES = 18
STEPS = 4
SPACING = 0.43
CUTOFF = 1.1
SIGMA = 0.41
COULOMB = 138.935458 / 15.0
MASS = 72.0
TIME_STEP = 0.02

MESH = pl.DeviceIdType.MESH
ROWS = 16
LANES = 128
HALO = 8
NONE = 31
SIDES = [(-1, -1), (-1, 0), (-1, 1), (0, -1), (0, 1), (1, -1), (1, 0), (1, 1)]
ZONES = [(0, 0), (1, 0), (0, 1), (1, 1)]
NEAR = [(dx, dy) for dy in range(-2, 3) for dx in range(-2, 3) if 0 < dx * dx + dy * dy <= 4]
MIDDLE = [(dx, dy) for dy in range(-2, 3) for dx in range(-2, 3) if dx * dx + dy * dy == 5]
FAR = [(dx, dy) for dy in range(-2, 3) for dx in range(-2, 3) if dx * dx + dy * dy == 8]
SHIFTS = NEAR + MIDDLE + FAR + [(0, 0)]
RUNS = [
    (0, len(NEAR), (-2, -1, 0, 1, 2), 0),
    (len(NEAR), len(MIDDLE), (-1, 0, 1), 5 * len(NEAR)),
    (len(NEAR) + len(MIDDLE), len(FAR), (0,), 5 * len(NEAR) + 3 * len(MIDDLE)),
    (len(SHIFTS) - 1, 1, (-2, -1, 1, 2), 5 * len(NEAR) + 3 * len(MIDDLE) + len(FAR)),
]
COUNT = RUNS[3][3] + 4
UNIT = SIGMA * 2.0 ** (1.0 / 6.0)
REACH = (CUTOFF / UNIT) ** 2
TAPER = (UNIT / CUTOFF) ** 4
LJ_FACTOR = 12.0 / UNIT**2 * TAPER
Q_FACTOR = COULOMB / UNIT**3 * TAPER
Q_SHIFT = (UNIT / CUTOFF) ** 3
AHEAD = 3


def lane_gather(values, index):
    return jnp.take_along_axis(values, index, axis=1)


def kernel(
    n_gx, n_gy, side,
    pos_ref, vel_ref, kind_ref, tile_ref, eps_ref, charge_ref,
    out_pos_ref, out_vel_ref,
    tile_send, tile_recv, send, recv, ext, kind_ext, charge_ext, coef_lj, coef_q, now, speed, mix, site_ref, square, eps_own,
    tile_sems, send_sems, recv_sems,
):
    width = side * SPACING
    my_x = lax.axis_index("gx")
    my_y = lax.axis_index("gy")

    def at(sx, sy):
        return (
            lax.rem(my_x + (sx + n_gx), n_gx),
            lax.rem(my_y + (sy + n_gy), n_gy),
        )

    barrier = pltpu.get_barrier_semaphore()
    for sx, sy in SIDES:
        pl.semaphore_signal(barrier, inc=1, device_id=at(sx, sy), device_id_type=MESH)

    lane = lax.broadcasted_iota(jnp.int32, (ROWS, LANES), 1)
    row = lax.broadcasted_iota(jnp.int32, (ROWS, LANES), 0)
    lane8 = lane[:8]
    half = lane >> 6
    y_site = (lane >> 3) & 7
    x_site = lane & 7
    low_half = lane8 < 64

    tile_send[...] = jnp.full((8, LANES), NONE - 1, jnp.int32)
    tile_send[0:2, 0 : tile_ref.shape[1]] = tile_ref[...]

    cluster = row
    sx_f = jnp.floor(pos_ref[0] * (1.0 / SPACING) + 0.5)
    sy_f = jnp.floor(pos_ref[1] * (1.0 / SPACING) + 0.5)
    sz_f = jnp.floor(pos_ref[2] * (1.0 / SPACING) + 0.5)
    site = (
        (sz_f.astype(jnp.int32) - 2 * cluster) * 64
        + sy_f.astype(jnp.int32) * 8
        + sx_f.astype(jnp.int32)
    )
    site = jnp.clip(site, 0, LANES - 1)
    site_ref[...] = site
    big_row = lax.broadcasted_iota(jnp.int32, (LANES, LANES), 0)
    row8 = row[:8]
    parts = []
    for part in range(2):
        total = jnp.zeros((8, LANES), jnp.float32)
        for sub in range(8):
            here = site[part * 8 + sub : part * 8 + sub + 1, :]
            onehot = jnp.where(big_row == here, 1.0, 0.0).astype(jnp.bfloat16)
            left = jnp.where(row8 == sub, lane8, 0).astype(jnp.float32).astype(jnp.bfloat16)
            total = total + lax.dot_general(
                left, onehot, (((1,), (1,)), ((), ())), preferred_element_type=jnp.float32
            )
        parts.append(total)
    slot = jnp.concatenate(parts, axis=0).astype(jnp.int32)

    def to_lattice(values):
        ordered = lane_gather(values, slot)
        first, second = ordered[:8], ordered[8:]
        even = jnp.where(low_half, first, pltpu.roll(second, 64, 1))
        odd = jnp.where(low_half, pltpu.roll(first, 64, 1), second)
        mix[pl.ds(0, 8, stride=2), :] = even
        mix[pl.ds(1, 8, stride=2), :] = odd
        return mix[...]

    def to_slots(values):
        mix[...] = values
        even = mix[pl.ds(0, 8, stride=2), :]
        odd = mix[pl.ds(1, 8, stride=2), :]
        first = jnp.where(low_half, even, pltpu.roll(odd, 64, 1))
        second = jnp.where(low_half, pltpu.roll(even, 64, 1), odd)
        return lane_gather(jnp.concatenate([first, second], axis=0), site_ref[...])

    for component in range(3):
        now[component] = to_lattice(pos_ref[component])
        speed[component] = to_lattice(vel_ref[component])
    kind = to_lattice(kind_ref[...].astype(jnp.float32))

    def pack_index(sx, sy):
        if sx != 0 and sy != 0:
            slot_of = lane >> 3
            inner = lane & 7
            zh, yb, xb = inner >> 2, (inner >> 1) & 1, inner & 1
        elif sx != 0:
            slot_of = lane >> 5
            inner = lane & 31
            zh, yb, xb = inner >> 4, (inner >> 1) & 7, inner & 1
        else:
            slot_of = lane >> 5
            inner = lane & 31
            zh, yb, xb = inner >> 4, (inner >> 3) & 1, inner & 7
        x_low = side - 2 if sx > 0 else 0
        y_low = side - 2 if sy > 0 else 0
        return slot_of, zh * 64 + (yb + y_low) * 8 + xb + x_low

    def unpack_index(sx, sy):
        if sx != 0 and sy != 0:
            return half * 4 + (y_site & 1) * 2 + (x_site & 1), 8
        if sx != 0:
            return half * 16 + y_site * 2 + (x_site & 1), 32
        return half * 16 + (y_site & 1) * 8 + x_site, 32

    def pack(values, sx, sy):
        slot_of, source = pack_index(sx, sy)
        packed = lane_gather(values[0], source)
        for component in range(1, len(values)):
            packed = jnp.where(slot_of == component, lane_gather(values[component], source), packed)
        return packed

    def side_copy(turn, number):
        sx, sy = SIDES[number]
        return pltpu.make_async_remote_copy(
            src_ref=send.at[turn, number],
            dst_ref=recv.at[turn, number],
            send_sem=send_sems.at[turn, number],
            recv_sem=recv_sems.at[turn, number],
            device_id=at(sx, sy),
            device_id_type=MESH,
        )

    def tile_copy(number):
        sx, sy = ZONES[number + 1]
        return pltpu.make_async_remote_copy(
            src_ref=tile_send,
            dst_ref=tile_recv.at[number],
            send_sem=tile_sems.at[0, number],
            recv_sem=tile_sems.at[1, number],
            device_id=at(sx, sy),
            device_id_type=MESH,
        )

    def image(turn, ux, uy, component):
        number = SIDES.index((-ux, -uy))
        index, stride = unpack_index(ux, uy)
        return lane_gather(recv[turn, number], index + component * stride)

    def merge_and_shift(images, dx, dy):
        merged = images[(0, 0)]
        in_x = (x_site < dx) if dx > 0 else (x_site >= side + dx)
        in_y = (y_site < dy) if dy > 0 else (y_site >= side + dy)
        ux = (dx > 0) - (dx < 0)
        uy = (dy > 0) - (dy < 0)
        if dx != 0:
            merged = jnp.where(in_x, images[(ux, 0)], merged)
        if dy != 0:
            outer = images[(0, uy)]
            if dx != 0:
                outer = jnp.where(in_x, images[(ux, uy)], outer)
            merged = jnp.where(in_y, outer, merged)
        if dx == 0 and dy == 0:
            return merged
        source = half * 64 + ((y_site + dy) & 7) * 8 + ((x_site + dx) & 7)
        return lane_gather(merged, source)

    def put_extended(ref, values):
        ref[pl.ds(HALO, ROWS), :] = values
        turned = pltpu.roll(jnp.where(row8 < 4, values[:8], values[8:]), 64, 1)
        ref[pl.ds(0, HALO), :] = turned
        ref[pl.ds(HALO + ROWS, HALO), :] = turned

    def gather_images(turn, component, own):
        images = {(0, 0): own}
        for ux, uy in SIDES:
            got = image(turn, ux, uy, component)
            if component == 0 and ux != 0:
                got = got + ux * width
            if component == 1 and uy != 0:
                got = got + uy * width
            images[(ux, uy)] = got
        return images

    def exchange(turn, values):
        for number, (sx, sy) in enumerate(SIDES):
            send[turn, number] = pack(values, sx, sy)
        for number in range(len(SIDES)):
            side_copy(turn, number).start()

    def spread_position(images, number):
        dx, dy = SHIFTS[number]
        for component in range(3):
            put_extended(ext.at[number, component], merge_and_shift(images[component], dx, dy))

    square[...] = jnp.zeros((LANES, LANES), jnp.float32)
    square[0:NTYPES, 0:NTYPES] = eps_ref[...]
    padded = square[...]
    square[...] = (padded + padded.T) * (0.5 * LJ_FACTOR)
    mix[0:1, :] = jnp.zeros((1, LANES), jnp.float32)
    mix[0:1, 0:NTYPES] = charge_ref[...]
    charge_row = jnp.broadcast_to(mix[0:1, :], (ROWS, LANES))

    pl.semaphore_wait(barrier, len(SIDES))
    own = [now[component] for component in range(3)]
    exchange(0, own + [kind])
    for number in range(3):
        tile_copy(number).start()
    for number in range(len(SIDES)):
        side_copy(0, number).wait_recv()
    for number in range(3):
        tile_copy(number).wait_recv()

    iota_small = lax.broadcasted_iota(jnp.int32, (32, LANES), 0)
    lane_small = lax.broadcasted_iota(jnp.int32, (32, LANES), 1)
    count_row = lax.broadcasted_iota(jnp.int32, (ROWS, 32), 0)
    count_lane = lax.broadcasted_iota(jnp.int32, (ROWS, 32), 1)
    nt = (((1,), (1,)), ((), ()))

    def onehot_of(condition):
        return jnp.where(condition, 1.0, 0.0).astype(jnp.bfloat16)

    tables = []
    for pair in range(2):
        table = jnp.zeros((ROWS, LANES), jnp.float32)
        for zone in (2 * pair, 2 * pair + 1):
            source = tile_send if zone == 0 else tile_recv.at[zone - 1]
            first = source[0:1, :]
            second = source[1:2, :]
            base = 32 * (zone & 1)
            small_a = onehot_of(iota_small == first)
            small_b = onehot_of(iota_small == second)
            place = big_row - base
            big_a = onehot_of((place == first) | (place == first + 64))
            big_b = onehot_of((place == second) | (place == second + 64))
            forth = lax.dot_general(small_a, big_b, nt, preferred_element_type=jnp.float32)
            back = lax.dot_general(small_b, big_a, nt, preferred_element_type=jnp.float32)
            on_diagonal = (lane_small & 63) == iota_small + base
            counts = jnp.where(on_diagonal, forth, forth + back).astype(jnp.bfloat16)
            picked = []
            for zh in range(2):
                layer = zh * ROWS + count_row
                if zone == 0:
                    which = layer >> 1
                elif zone == 1:
                    which = 16 + (layer >> 3)
                elif zone == 2:
                    which = 20 + (layer >> 3)
                else:
                    which = jnp.full_like(layer, 24)
                picked.append(
                    jnp.dot(onehot_of(count_lane == which), counts, preferred_element_type=jnp.float32)
                )
            table = table + jnp.where(half == 0, picked[0], picked[1])
        tables.append(table)

    cat_x, cat_y = (lane >> 2) & 3, lane & 3
    weight_of = {}
    for dz in range(-2, 3):
        layer = half * ROWS + row + dz
        in_z = (layer >= 0) & (layer < 2 * ROWS)
        total = jnp.zeros((ROWS, LANES), jnp.float32)
        for zone, (ox, oy) in enumerate(ZONES):
            on_x = (cat_x >= 2) if ox else (cat_x <= 2)
            on_y = (cat_y >= 2) if oy else (cat_y <= 2)
            in_x = cat_x == (2 if ox else 1)
            in_y = cat_y == (2 if oy else 1)
            start = jnp.where(in_x, jnp.where(in_y, 24, 16), jnp.where(in_y, 20, 0))
            shift = jnp.where(in_x, jnp.where(in_y, 6, 3), jnp.where(in_y, 3, 1))
            which = jnp.where(on_x & on_y & in_z, start + (layer >> shift), NONE)
            total = total + lane_gather(tables[zone >> 1], half * 64 + 32 * (zone & 1) + which)
        weight_of[dz] = total

    def category(site, step):
        other = site + step
        return jnp.where(
            other >= side, 1, jnp.where(other < 0, 3, jnp.where((site < 2) & (other < 2), 2, 0))
        )

    kind_images = gather_images(0, 3, kind)
    kind_images = {key: value.astype(jnp.int32) for key, value in kind_images.items()}
    charge_images = {key: lane_gather(charge_row, value) for key, value in kind_images.items()}
    kind_own = kind_images[(0, 0)]
    for k in range(NTYPES):
        row_k = jnp.broadcast_to(square[k : k + 1, :], (ROWS, LANES))
        eps_own[k] = lane_gather(row_k, kind_own)

    def depth_of(other):
        level = [eps_own[k] for k in range(NTYPES)] + [jnp.zeros((ROWS, LANES), jnp.float32)]
        bit = 1
        while len(level) > 1:
            odd = (other & bit) != 0
            joined = [jnp.where(odd, level[k + 1], level[k]) for k in range(0, len(level) - 1, 2)]
            if len(level) % 2:
                joined.append(level[-1])
            level = joined
            bit = 2 * bit
        return level[0]

    def spread_kind(number):
        dx, dy = SHIFTS[number]
        put_extended(kind_ext.at[number], merge_and_shift(kind_images, dx, dy))
        put_extended(charge_ext.at[number], merge_and_shift(charge_images, dx, dy))

    for number in range(AHEAD):
        spread_kind(number)
    charge_own = charge_images[(0, 0)] * Q_FACTOR
    for first, length, depths, base in RUNS:
        for sub in range(length):
            number = first + sub
            if number + AHEAD < len(SHIFTS):
                spread_kind(number + AHEAD)
            dx, dy = SHIFTS[number]
            chosen = half * 64 + category(x_site, dx) * 4 + category(y_site, dy)
            for turn, dz in enumerate(depths):
                place = base + sub * len(depths) + turn
                weight = lane_gather(weight_of[dz], chosen)
                rows = pl.ds(HALO + dz, ROWS)
                depth = depth_of(kind_ext[number, rows, :])
                coef_lj[place] = weight * depth
                coef_q[place] = weight * (charge_own * charge_ext[number, rows, :])

    def add_pair(scaled, force, place, number, dz):
        apart = [scaled[k] - ext[number, k, pl.ds(HALO + dz, ROWS), :] for k in range(3)]
        dist_sq = apart[0] * apart[0] + apart[1] * apart[1] + apart[2] * apart[2]
        inv_r = lax.rsqrt(dist_sq)
        inv_sq = inv_r * inv_r
        taper = jnp.maximum(REACH - dist_sq, 0.0)
        inv_4 = inv_sq * inv_sq
        inv_6 = inv_4 * inv_sq
        lennard = coef_lj[place] * (inv_4 * inv_4) * (inv_6 - 1.0)
        coulomb = coef_q[place] * (inv_sq * inv_r - Q_SHIFT)
        scalar = taper * taper * (lennard + coulomb)
        return [force[k] + scalar * apart[k] for k in range(3)]

    def advance(turn):
        mine = [now[component] for component in range(3)]
        images = []
        for component in range(3):
            found = gather_images(turn, component, mine[component])
            images.append({key: value * (1.0 / UNIT) for key, value in found.items()})
        scaled = [images[k][(0, 0)] for k in range(3)]
        force = [jnp.zeros((ROWS, LANES), jnp.float32) for _ in range(3)]
        for number in range(AHEAD):
            spread_position(images, number)
        for first, length, depths, base in RUNS:
            for sub in range(length):
                number = first + sub
                if number + AHEAD < len(SHIFTS):
                    spread_position(images, number + AHEAD)
                for which, dz in enumerate(depths):
                    force = add_pair(scaled, force, base + sub * len(depths) + which, number, dz)
        for k in range(3):
            new_speed = speed[k] + (TIME_STEP / MASS * UNIT) * force[k]
            speed[k] = new_speed
            now[k] = mine[k] + TIME_STEP * new_speed

    def turn_body(turn, carry):
        advance(turn)
        exchange(turn + 1, [now[component] for component in range(3)])
        for number in range(len(SIDES)):
            side_copy(turn + 1, number).wait_recv()
        return carry

    lax.fori_loop(0, STEPS - 1, turn_body, 0)
    advance(STEPS - 1)
    for component in range(3):
        out_pos_ref[component] = to_slots(now[component])
        out_vel_ref[component] = to_slots(speed[component])
    for turn in range(STEPS):
        for number in range(len(SIDES)):
            side_copy(turn, number).wait_send()
    for number in range(3):
        tile_copy(number).wait_send()


def per_device(n_gx, n_gy, positions, velocities, bead_types, eps_table, charges, x_list, y_list, tiles):
    beads = positions.shape[-1]
    strip = x_list.shape[-1]
    side = 2 * beads // strip
    shape = jax.ShapeDtypeStruct((3, ROWS, LANES), jnp.float32)
    vmem = pl.BlockSpec(memory_space=pltpu.VMEM)
    new_pos, new_vel = pl.pallas_call(
        functools.partial(kernel, n_gx, n_gy, side),
        out_shape=(shape, shape),
        in_specs=[vmem] * 6,
        out_specs=(vmem, vmem),
        scratch_shapes=[
            pltpu.VMEM((8, LANES), jnp.int32),
            pltpu.VMEM((3, 8, LANES), jnp.int32),
            pltpu.VMEM((STEPS, len(SIDES), ROWS, LANES), jnp.float32),
            pltpu.VMEM((STEPS, len(SIDES), ROWS, LANES), jnp.float32),
            pltpu.VMEM((len(SHIFTS), 3, ROWS + 2 * HALO, LANES), jnp.float32),
            pltpu.VMEM((len(SHIFTS), ROWS + 2 * HALO, LANES), jnp.int32),
            pltpu.VMEM((len(SHIFTS), ROWS + 2 * HALO, LANES), jnp.float32),
            pltpu.VMEM((COUNT, ROWS, LANES), jnp.float32),
            pltpu.VMEM((COUNT, ROWS, LANES), jnp.float32),
            pltpu.VMEM((3, ROWS, LANES), jnp.float32),
            pltpu.VMEM((3, ROWS, LANES), jnp.float32),
            pltpu.VMEM((ROWS, LANES), jnp.float32),
            pltpu.VMEM((ROWS, LANES), jnp.int32),
            pltpu.VMEM((LANES, LANES), jnp.float32),
            pltpu.VMEM((NTYPES, ROWS, LANES), jnp.float32),
            pltpu.SemaphoreType.DMA((2, 3)),
            pltpu.SemaphoreType.DMA((STEPS, len(SIDES))),
            pltpu.SemaphoreType.DMA((STEPS, len(SIDES))),
        ],
        compiler_params=pltpu.CompilerParams(collective_id=0, has_side_effects=True),
    )(
        positions.reshape(3, ROWS, LANES),
        velocities.reshape(3, ROWS, LANES),
        bead_types.reshape(ROWS, LANES),
        tiles.reshape(2, -1),
        eps_table,
        charges[None],
    )
    return new_pos.reshape(positions.shape), new_vel.reshape(velocities.shape)


def solution(mesh):
    return jax.shard_map(
        functools.partial(per_device, mesh.shape["gx"], mesh.shape["gy"]),
        mesh=mesh,
        in_specs=(
            P(None, "gx", "gy", None),
            P(None, "gx", "gy", None),
            P("gx", "gy", None),
            P(),
            P(),
            P("gx", "gy", None),
            P("gx", "gy", None),
            P("gx", "gy", None, None),
        ),
        out_specs=(P(None, "gx", "gy", None), P(None, "gx", "gy", None)),
        check_vma=False,
    )
```
